32 devices in a mesh: curve: 8 (over z, x), sub: 4 (over y, core).
Axes of the slice: x: 2, y: 2, z: 4, core: 2. Of those that a mesh axis runs over, the one named last changes fastest.
Arguments:
- direction: float32 [8, 4096], P(None, ('curve', 'sub')), may hold values from -6 to 6
- base_velocity: float32 [3, 16384], P(None, ('curve', 'sub')), may hold values from -6 to 6
- weight: float32 [3, 16384], P(None, ('curve', 'sub')), may hold values from 0.3 to 3
- element_matrix: float32 [81, 81, 4096], P(None, None, ('curve', 'sub')), as said below
- connectivity: int32 [27, 4096], P(None, ('curve', 'sub')), may hold values from 384 to 1151, as said below
- element_count: int32 [32], P(('curve', 'sub')), may hold values from 64 to 128
- basal_owner: int32 [8192], P(('curve', 'sub')), may hold values from 0 to 511
Outputs:
- gradient: float32 [8, 4096], P(None, ('curve', 'sub'))
- adjoint_field: float32 [3, 8, 16384], P(None, None, ('curve', 'sub'))
The draws below stay inside these ranges and needn't reach their ends.
Inputs may be any that keep to these rules, and one draw needn't show every extreme that they name: `connectivity`: device 0 has no corner below 512 and the last device none at or above 1024. A corner below 512 is at or above 384; a corner at or above 1024 is below 1152. `element_matrix`: Symmetric.
All inputs are finite; a program needn't handle non-finite values.
Results may differ from the reference program's by a relative error of at most 0.00016.
Values sent between devices are 32-bit elements; how exact they have to be, the bound alone decides.
No kernel may reach another device: no remote copies, remote signals or barrier semaphores. Data moves between devices by JAX's collectives and lax.ppermute only.
A program may use at most 64 MiB of HBM per device.

```python
import math
import jax
import jax.numpy as jnp
from jax import lax

COMP = 3
E_DEV = 128
NODE_DEV = 512
BAND = 128
NRHS = 8
BASAL_DEV = 256
NODES = 16384
B_TOTAL = 8192
PARAMS = 4096
GROUP_PARAMS = 512
N_CURVE = 8
N_SUB = 4


def draw_element_matrix(key, part):
    total = E_DEV * N_CURVE * N_SUB
    key_a, key_b = jax.random.split(jax.random.fold_in(key, 11))
    raw = jax.random.normal(key_a, (81, 81, total), jnp.float32)
    sym = (raw + jnp.transpose(raw, (1, 0, 2))) / 18.0
    diag = jax.random.uniform(key_b, (81, total), jnp.float32, 1.0, 2.0)
    eye = jnp.eye(81, dtype=jnp.float32)
    return sym * (1.0 - eye)[:, :, None] + eye[:, :, None] * diag[None, :, :]


def draw_connectivity(key, part):
    devices = N_CURVE * N_SUB
    total = E_DEV * devices
    key_a, key_b, key_c = jax.random.split(jax.random.fold_in(key, 23), 3)
    region = jax.random.randint(key_a, (27, total), 0, 4)
    slot = jax.random.randint(key_b, (27, total), 0, NODE_DEV)
    edge = jax.random.randint(key_c, (27, total), 0, BAND)
    place = jnp.arange(total, dtype=jnp.int32)
    owner = (place // E_DEV)[None, :]
    local = (place % E_DEV)[None, :]
    to_prev = (region == 0) & (local < E_DEV // 4) & (owner > 0)
    to_next = (region == 0) & (local >= E_DEV // 4) & (local < E_DEV // 2) & (owner < devices - 1)
    value = NODE_DEV + slot
    value = jnp.where(to_prev, NODE_DEV - BAND + edge, value)
    value = jnp.where(to_next, 2 * NODE_DEV + edge, value)
    return value.astype(jnp.int32)


def draw_element_count(key, part):
    devices = N_CURVE * N_SUB
    key_a, key_b = jax.random.split(jax.random.fold_in(key, 37))
    counts = jax.random.randint(key_a, (devices,), E_DEV // 2, E_DEV + 1)
    pick = jax.random.randint(key_b, (), 0, devices)
    other = (pick + 1) % devices
    place = jnp.arange(devices, dtype=jnp.int32)
    counts = jnp.where(place == pick, E_DEV, counts)
    counts = jnp.where(place == other, E_DEV // 2, counts)
    return counts.astype(jnp.int32)


def with_ends(drawn, rng, least, top_value):
    extent = drawn.shape
    spot = [jax.random.randint(jax.random.fold_in(rng, axis), (), 0, extent[axis]) for axis in range(len(extent))]
    drawn = drawn.at[tuple(spot)].set(least)
    longest = extent.index(max(extent))
    spot[longest] = (spot[longest] + 1) % extent[longest]
    return drawn.at[tuple(spot)].set(top_value)


def shard_levels(key, extent, shards, smallest, top_value):
    def one(axis_at, blocks):
        heights = jax.random.uniform(jax.random.fold_in(jax.random.fold_in(key, 6), axis_at), (blocks,), jnp.float32, smallest / len(shards), top_value / len(shards))
        return jnp.repeat(jnp.exp(heights), extent[axis_at] // blocks).reshape((-1,) + (1,) * (len(extent) - axis_at - 1))

    factor_of = one(*shards[0])
    for cut in shards[1:]:
        factor_of = factor_of * one(*cut)
    return factor_of


def scatter_about(own_key, shape, width, most, cuts=(), kind=jnp.bfloat16):
    result = width * jax.random.normal(own_key, shape, jnp.float32)
    if cuts:
        result = result * shard_levels(own_key, shape, cuts, -0.22, 0.18)
    return jnp.clip(result, -most, most).astype(kind)


def setup_inputs(seed: int = 0) -> dict:
    splits = jax.random.split(jax.random.key(seed), 8)
    direction = scatter_about(splits[0], (NRHS, PARAMS), 1.0, 6.0, ((1, 32),), jnp.float32)
    base_velocity = scatter_about(splits[1], (COMP, NODES), 1.0, 6.0, ((1, 32),), jnp.float32)
    weight = jnp.clip(jnp.exp(math.log(3.0) - 2.3025851 * jax.random.uniform(splits[2], (COMP, NODES), jnp.float32) ** shard_levels(splits[2], (COMP, NODES), ((1, 32),), -0.2, 0.2)), 0.3, 3.0)
    element_matrix = draw_element_matrix(jax.random.fold_in(splits[7], 71), 0)
    connectivity = draw_connectivity(jax.random.fold_in(splits[7], 71), 0)
    element_count = draw_element_count(jax.random.fold_in(splits[7], 71), 0)
    basal_owner = with_ends(jax.random.randint(splits[6], (B_TOTAL,), 0, GROUP_PARAMS), jax.random.fold_in(splits[6], 1), 0, GROUP_PARAMS - 1).astype(jnp.int32)
    return dict(direction=direction, base_velocity=base_velocity, weight=weight, element_matrix=element_matrix, connectivity=connectivity, element_count=element_count, basal_owner=basal_owner)


def device_part(padded, kmat, conn, count, device):
    rhs = padded.shape[1]
    elems = conn.shape[1]
    ext = lax.dynamic_slice_in_dim(padded, (device * NODE_DEV).astype(jnp.int32), 3 * NODE_DEV, 2)
    flat = conn.reshape(-1)
    vals = jnp.take(ext, flat, axis=2).reshape(3, rhs, 27, elems)
    vals = vals.transpose(0, 2, 1, 3).reshape(81, rhs, elems)
    out = jnp.einsum("ije,jre->ire", kmat, vals, precision=lax.Precision.HIGHEST)
    live = (jnp.arange(elems) < count).astype(out.dtype)
    out = out * live
    out = out.reshape(3, 27, rhs, elems).transpose(0, 2, 1, 3).reshape(3, rhs, 27 * elems)
    return jnp.zeros((3, rhs, 3 * NODE_DEV), out.dtype).at[:, :, flat].add(out)


def assemble(field, element_matrix, connectivity, element_count):
    devices = N_CURVE * N_SUB
    zeros = jnp.zeros((3, field.shape[1], NODE_DEV), field.dtype)
    padded = jnp.concatenate([zeros, field, zeros], axis=2)

    def step(device, total):
        kmat = lax.dynamic_slice_in_dim(element_matrix, (device * E_DEV).astype(jnp.int32), E_DEV, 2)
        conn = lax.dynamic_slice_in_dim(connectivity, (device * E_DEV).astype(jnp.int32), E_DEV, 1)
        part = device_part(padded, kmat, conn, element_count[device], device)
        start = (device * NODE_DEV).astype(jnp.int32)
        old = lax.dynamic_slice_in_dim(total, start, 3 * NODE_DEV, 2)
        return lax.dynamic_update_slice_in_dim(total, old + part, start, 2)

    total = lax.fori_loop(jnp.int32(0), jnp.int32(devices), step, jnp.zeros_like(padded))
    return total[:, :, NODE_DEV:NODE_DEV + field.shape[2]]


def reference(direction, base_velocity, weight, element_matrix, connectivity, element_count, basal_owner):
    devices = N_CURVE * N_SUB
    rhs = direction.shape[0]
    basal_index = jnp.arange(BASAL_DEV * devices, dtype=jnp.int32)
    basal_device = basal_index // BASAL_DEV
    basal_node = basal_device * NODE_DEV + basal_index % BASAL_DEV
    basal_param = (basal_device // N_SUB) * GROUP_PARAMS + basal_owner
    beta = direction[:, basal_param]
    velocity = base_velocity[:, basal_node]
    nodes = base_velocity.shape[1]
    force = jnp.zeros((3, rhs, nodes), jnp.float32).at[:, :, basal_node].set(velocity[:, None, :] * beta[None])
    forward = assemble(force, element_matrix, connectivity, element_count)
    weighted = weight[:, None, :] * forward
    adjoint_field = assemble(weighted, element_matrix, connectivity, element_count)
    terms = jnp.sum(velocity[:, None, :] * adjoint_field[:, :, basal_node], axis=0)
    gradient = jnp.zeros((rhs, direction.shape[1]), jnp.float32).at[:, basal_param].add(terms)
    return gradient, adjoint_field
```

```python
import functools

import jax
import jax.numpy as jnp
from jax import lax
from jax.experimental import pallas as pl
from jax.experimental.pallas import tpu as pltpu
from jax.sharding import PartitionSpec as P

BAND = 128
LANE = 128
AX = ("curve", "sub")
VMEM = pl.BlockSpec(memory_space=pltpu.VMEM)
SMEM = pl.BlockSpec(memory_space=pltpu.SMEM)
f32 = jnp.float32


def params(mib):
    return pltpu.CompilerParams(vmem_limit_bytes=mib << 20)


def xor_order(subs):
    order, masks = [0], []
    while len(order) < subs:
        mask = 2 * len(order) - 1
        masks.append(mask)
        order = order + [mask ^ r for r in order]
    return order, masks


def chain_mask(step, masks):
    return masks[step]


def pack_kernel(direction, velocity, owner, out):
    out[0:8, :] = direction[...]
    out[8:11, :] = velocity[:, :BAND]
    out[11:12, :] = owner[:, :BAND].astype(f32)
    out[12:16, :] = jnp.zeros((4, LANE), f32)


def grow_kernel(held, got, out):
    dirs = held.shape[0] - 8
    out[0:dirs, :] = held[0:dirs, :]
    out[dirs : 2 * dirs, :] = got[0:dirs, :]
    out[2 * dirs : 2 * dirs + 8, :] = held[dirs : dirs + 8, :]


def rows8(row):
    return jnp.broadcast_to(row, (8, LANE))


def lanes_of(table, index):
    return jnp.take_along_axis(table, index, axis=1, mode="promise_in_bounds")


def lookup(owner_row, tables, shards):
    low = rows8(owner_row & (LANE - 1))
    high = rows8(owner_row >> 7)
    out = jnp.zeros((8, LANE), f32)
    for table, shard in zip(tables, shards):
        out = jnp.where(high == shard, lanes_of(table, low), out)
    return out


def gather_corners(field, blocks, conn, base, corners, v_ref):
    held = {(c, b): field(c, b) for c in range(3) for b in blocks}
    for n in range(corners):
        row = conn[n : n + 1, :] - base
        low = rows8(row & (LANE - 1))
        high = rows8(row >> 7)
        tests = {b: high == b for b in blocks}
        for c in range(3):
            acc = jnp.zeros((8, LANE), f32)
            for b in blocks:
                acc = jnp.where(tests[b], lanes_of(held[c, b], low), acc)
            v_ref[c * corners + n] = acc


def product(k_ref, v_ref, o_ref, count, size, group=9):
    live = (lax.broadcasted_iota(jnp.int32, (8, LANE), 1) < count).astype(f32)

    def step(i, carry):
        start = i * group
        acc = [jnp.zeros((8, LANE), f32) for _ in range(group)]
        for j in range(size):
            vj = v_ref[j]
            for t in range(group):
                acc[t] = acc[t] + rows8(k_ref[start + t, j : j + 1, :]) * vj
        for t in range(group):
            o_ref[start + t] = acc[t] * live
        return carry

    lax.fori_loop(0, size // group, step, 0)


def halves(x):
    high = x.astype(jnp.bfloat16).astype(f32)
    return high, x - high


def scatter_corners(o_ref, conn, base, corners, blocks, a_ref, one_ref):
    sub = lax.broadcasted_iota(jnp.int32, (LANE, LANE), 0)
    for n in range(corners):
        row = conn[n : n + 1, :] - base
        low = jnp.broadcast_to(row & (LANE - 1), (LANE, LANE))
        one_ref[:, n * LANE : (n + 1) * LANE] = (low == sub).astype(f32).astype(jnp.bfloat16)
        high = rows8(row >> 7)
        parts = [halves(o_ref[c * corners + n]) for c in range(3)]
        pieces = [p[0] for p in parts] + [p[1] for p in parts]
        for b in range(blocks):
            here = high == b
            stack = jnp.concatenate([jnp.where(here, p, 0.0) for p in pieces], axis=0)
            a_ref[b * 48 : (b + 1) * 48, n * LANE : (n + 1) * LANE] = stack.astype(jnp.bfloat16)
    res = lax.dot_general(
        a_ref[...], one_ref[...], (((1,), (1,)), ((), ())), preferred_element_type=f32
    )
    return [res[b * 48 : b * 48 + 24] + res[b * 48 + 24 : b * 48 + 48] for b in range(blocks)]


def pick(index, options):
    out = options[-1][1]
    for value, array in options[:-1]:
        out = jnp.where(index == value, array, out)
    return out


def forward_kernel(cfg, *refs):
    subs, order, masks, nodes, basal, corners = cfg
    steps = len(masks)
    held, got, (low_b, mid_b) = refs[0], refs[1 : 1 + steps], refs[1 + steps : 3 + steps]
    velocity, owner, weight, kmat, conn, count = refs[3 + steps : 9 + steps]
    ext, m0, m1, info_out = refs[9 + steps : 13 + steps]
    v_ref, o_ref, a_ref, one_ref = refs[13 + steps :]
    s = lax.axis_index("sub")
    half = subs // 2
    own_blocks = nodes // LANE
    blocks = own_blocks + 2
    last = s == subs - 1
    dirs = 8 * half

    info = low_b[dirs : dirs + 8, :]
    for t in range(steps):
        rows = got[t].shape[0]
        chain = (s & (2 * (1 << t) - 1)) == (1 << t) - 1
        info = jnp.where(chain, got[t][rows - 8 : rows, :], info)
    info = jnp.where(last, low_b[dirs : dirs + 8, :], info)
    info_out[...] = info

    mine = [held[8 * q : 8 * q + 8, :] for q in range(half)]
    mine += [got[-1][8 * q : 8 * q + 8, :] for q in range(half)]
    shards = [s ^ r for r in order]
    theirs = [low_b[8 * q : 8 * q + 8, :] for q in range(half)]
    theirs += [mid_b[8 * q : 8 * q + 8, :] for q in range(half)]
    their_shards = [order[q] for q in range(half)] + [half ^ order[q] for q in range(half)]
    next_tables = [jnp.where(last, b, a) for a, b in zip(mine, theirs)]
    next_shards = [jnp.where(last, b, a) for a, b in zip(shards, their_shards)]

    values = {}
    for b in range(basal // LANE):
        beta = lookup(owner[:, b * LANE : (b + 1) * LANE], mine, shards)
        for c in range(3):
            values[c, 1 + b] = rows8(velocity[c : c + 1, b * LANE : (b + 1) * LANE]) * beta
    beta = lookup(info[3:4, :].astype(jnp.int32), next_tables, next_shards)
    for c in range(3):
        values[c, blocks - 1] = rows8(info[c : c + 1, :]) * beta
    live_blocks = [1 + b for b in range(basal // LANE)] + [blocks - 1]
    base = nodes - BAND
    gather_corners(lambda c, b: values[c, b], live_blocks, conn, base, corners, v_ref)
    product(kmat, v_ref, o_ref, count[0], 3 * corners)
    sums = scatter_corners(o_ref, conn, base, corners, blocks, a_ref, one_ref)
    for b in range(blocks):
        ext[:, b * LANE : (b + 1) * LANE] = sums[b]
    even = (s & 1) == 0
    before = jnp.concatenate([sums[0], sums[1]], axis=1)
    after = jnp.concatenate([sums[blocks - 2], sums[blocks - 1]], axis=1)
    m0[0:24, :] = jnp.where(even, after, before)
    m1[0:24, :] = jnp.where(even, before, after)
    pad = jnp.zeros((5, LANE), f32)
    none = jnp.zeros((8, LANE), f32)
    w_low = jnp.concatenate([weight[:, 0:BAND], pad], axis=0)
    w_high = jnp.concatenate([weight[:, nodes - BAND : nodes], pad], axis=0)
    before = jnp.concatenate([none, w_low], axis=1)
    after = jnp.concatenate([w_high, none], axis=1)
    m0[24:32, :] = jnp.where(even, after, before)
    m1[24:32, :] = jnp.where(even, before, after)


def adjoint_kernel(cfg, *refs):
    subs, order, masks, nodes, basal, corners = cfg
    ext, r0, r1, info, velocity, owner, weight, kmat, conn, count = refs[:10]
    n_out = 4 + len(masks)
    outs = refs[10 : 10 + n_out]
    v_ref, o_ref, a_ref, one_ref = refs[10 + n_out :]
    own_out, swap_out, edge_out, mid_out = outs[:4]
    dense_out = outs[4]
    band_outs = outs[5:]
    s = lax.axis_index("sub")
    half = subs // 2
    blocks = nodes // LANE + 2
    last = s == subs - 1
    even = (s & 1) == 0
    base = nodes - BAND

    prev = jnp.where(even, r1[...], r0[...])
    nxt = jnp.where(even, r0[...], r1[...])

    values = {}
    for c in range(3):
        part = slice(8 * c, 8 * c + 8)
        for b in range(blocks):
            x = ext[part, b * LANE : (b + 1) * LANE]
            if b == 0:
                x = (x + prev[part, 0:LANE]) * rows8(prev[24 + c : 25 + c, 0:LANE])
            elif b == blocks - 1:
                x = (x + nxt[part, LANE:]) * rows8(nxt[24 + c : 25 + c, LANE:])
            else:
                if b == 1:
                    x = x + prev[part, LANE:]
                if b == blocks - 2:
                    x = x + nxt[part, 0:LANE]
                x = x * rows8(weight[c : c + 1, (b - 1) * LANE : b * LANE])
            values[c, b] = x
    gather_corners(lambda c, b: values[c, b], range(blocks), conn, base, corners, v_ref)
    product(kmat, v_ref, o_ref, count[0], 3 * corners)
    sums = scatter_corners(o_ref, conn, base, corners, blocks, a_ref, one_ref)
    for b in range(1, blocks - 1):
        own_out[:, (b - 1) * LANE : b * LANE] = sums[b]
    lower, upper = sums[0], sums[blocks - 1]

    n_basal = basal // LANE
    terms, owners = [], []
    for b in range(n_basal):
        terms.append(
            sum(
                rows8(velocity[c : c + 1, b * LANE : (b + 1) * LANE]) * sums[1 + b][8 * c : 8 * c + 8]
                for c in range(3)
            )
        )
        owners.append(owner[:, b * LANE : (b + 1) * LANE])
    beyond = sum(rows8(info[c : c + 1, :]) * upper[8 * c : 8 * c + 8] for c in range(3))
    terms.append(jnp.where(last, 0.0, beyond))
    owners.append(info[3:4, :].astype(jnp.int32))
    across = jnp.where(last, beyond, 0.0)
    sub_iota = lax.broadcasted_iota(jnp.int32, (LANE, LANE), 0)
    one = jnp.concatenate(
        [
            (jnp.broadcast_to(o & (LANE - 1), (LANE, LANE)) == sub_iota).astype(f32).astype(jnp.bfloat16)
            for o in owners
        ],
        axis=1,
    )
    split = [halves(t) for t in terms]
    split_across = halves(across)
    zero = jnp.zeros((8, LANE), f32)
    lines = []
    for r in order:
        here = [rows8(o >> 7) == (s ^ r) for o in owners]
        for piece in range(2):
            lines.append(
                jnp.concatenate([jnp.where(h, t[piece], 0.0) for h, t in zip(here, split)], axis=1)
            )
    for q in range(subs):
        shard = order[q] if q < half else half ^ order[q - half]
        here = rows8(owners[-1] >> 7) == shard
        for piece in range(2):
            lines.append(
                jnp.concatenate(
                    [zero] * n_basal + [jnp.where(here, split_across[piece], 0.0)], axis=1
                )
            )
    res = lax.dot_general(
        jnp.concatenate(lines, axis=0).astype(jnp.bfloat16),
        one,
        (((1,), (1,)), ((), ())),
        preferred_element_type=f32,
    )
    dense = [res[16 * q : 16 * q + 8] + res[16 * q + 8 : 16 * q + 16] for q in range(2 * subs)]
    rows = 8 * half
    for q in range(half):
        dense_out[8 * q : 8 * q + 8, :] = dense[q]
        swap_out[8 * q : 8 * q + 8, :] = dense[half + q]
        edge_out[8 * q : 8 * q + 8, :] = dense[subs + q]
        mid_out[8 * q : 8 * q + 8, :] = dense[subs + half + q]
    edge_out[rows : rows + 24, :] = jnp.where(last, upper, lower)
    up = (s & half) == 0
    swap_out[rows : rows + 24, :] = jnp.where(up, upper, lower)
    for t, band in enumerate(band_outs):
        up = (s & (1 << t)) == 0
        band[...] = jnp.where(up, upper, lower)


def shrink_kernel(first, *refs):
    if first:
        held, got, edge, mid, band, msg, left = refs
    else:
        held, got, band, msg, left = refs
    rows = held.shape[0]
    total = held[...] + got[0:rows, :]
    if first:
        total = total + edge[0:rows, :] + mid[...]
    keep = rows // 2
    left[...] = total[0:keep]
    msg[0:keep, :] = total[keep:]
    msg[keep : keep + 24, :] = band[...]


def finish_kernel(cfg, *refs):
    subs, order, masks, nodes, basal, corners = cfg
    steps = len(masks)
    own, held, edge = refs[:3]
    got = refs[3 : 3 + steps]
    gradient, field = refs[3 + steps :]
    s = lax.axis_index("sub")
    gradient[...] = held[...] + got[0][0:8, :]
    bands = [g[g.shape[0] - 24 :, :] for g in got]
    prev = edge[edge.shape[0] - 24 :, :]
    nxt = prev
    for t in range(steps):
        ones = (1 << t) - 1
        nxt = jnp.where((s & (2 * ones + 1)) == ones, bands[t], nxt)
        prev = jnp.where((s & (2 * ones + 1)) == ones + 1, bands[t], prev)
    field[:, 0:LANE] = own[:, 0:LANE] + prev
    field[:, LANE : nodes - LANE] = own[:, LANE : nodes - LANE]
    field[:, nodes - LANE :] = own[:, nodes - LANE :] + nxt


def shape(*dims):
    return jax.ShapeDtypeStruct(dims, f32)


def local(curves, subs, direction, base_velocity, weight, element_matrix, connectivity, element_count, basal_owner):
    order, masks = xor_order(subs)
    total = curves * subs
    half = subs // 2
    nodes = base_velocity.shape[1]
    basal = basal_owner.shape[0]
    corners, elems = connectivity.shape
    size = 3 * corners
    blocks = nodes // LANE + 2
    cfg = (subs, order, masks, nodes, basal, corners)
    owner = basal_owner.reshape(1, basal)

    def call(kernel, out_shape, scratch=(), mib=4, specs=None):
        def run(*args):
            return pl.pallas_call(
                kernel,
                out_shape=out_shape,
                in_specs=specs or [VMEM] * len(args),
                out_specs=jax.tree.map(lambda _: VMEM, out_shape),
                scratch_shapes=list(scratch),
                compiler_params=params(mib),
            )(*args)

        return run

    def swap_sub(x, mask):
        return lax.ppermute(x, "sub", [(i, i ^ mask) for i in range(subs)])

    edges = [(subs * g + subs - 1, subs * (g + 1)) for g in range(curves - 1)]

    held = call(pack_kernel, shape(16, LANE))(direction, base_velocity, owner)
    got = []
    for mask in masks[:-1]:
        got.append(swap_sub(held, mask))
        rows = 2 * held.shape[0] - 8
        held = call(grow_kernel, shape(rows, LANE))(held, got[-1])
    got.append(swap_sub(held, masks[-1]))
    low_b = lax.ppermute(held, AX, [(b, a) for a, b in edges])
    mid_b = lax.ppermute(held, AX, [(b + half, a) for a, b in edges])

    scratch = [
        pltpu.VMEM((size, 8, LANE), f32),
        pltpu.VMEM((size, 8, LANE), f32),
        pltpu.VMEM((48 * blocks, corners * LANE), jnp.bfloat16),
        pltpu.VMEM((LANE, corners * LANE), jnp.bfloat16),
    ]
    ext, m0, m1, info = call(
        functools.partial(forward_kernel, cfg),
        (shape(24, blocks * LANE), shape(32, 2 * LANE), shape(32, 2 * LANE), shape(8, LANE)),
        scratch,
        16,
        [VMEM] * (8 + len(got)) + [SMEM],
    )(held, *got, low_b, mid_b, base_velocity, owner, weight, element_matrix, connectivity, element_count)

    r0 = lax.ppermute(m0, AX, [p for i in range(0, total - 1, 2) for p in ((i, i + 1), (i + 1, i))])
    r1 = lax.ppermute(m1, AX, [p for i in range(1, total - 1, 2) for p in ((i, i + 1), (i + 1, i))])

    steps = len(masks)
    rows = 8 * half
    own, swap_msg, edge_msg, mid_msg, dense, *bands = call(
        functools.partial(adjoint_kernel, cfg),
        (shape(24, nodes), shape(rows + 24, LANE), shape(rows + 24, LANE), shape(rows, LANE), shape(rows, LANE))
        + (shape(24, LANE),) * (steps - 1),
        scratch,
        16,
        [VMEM] * 9 + [SMEM],
    )(ext, r0, r1, info, base_velocity, owner, weight, element_matrix, connectivity, element_count)

    by_mask = [None] * steps
    by_mask[-1] = swap_sub(swap_msg, masks[-1])
    edge = lax.ppermute(edge_msg, AX, [p for a, b in edges for p in ((a, b), (b, a))])
    mid = lax.ppermute(mid_msg, AX, [(a, b + half) for a, b in edges])
    extra = (edge, mid)
    for t in range(steps - 2, -1, -1):
        keep = dense.shape[0] // 2
        msg, dense = call(
            functools.partial(shrink_kernel, bool(extra)), (shape(keep + 24, LANE), shape(keep, LANE))
        )(dense, by_mask[t + 1], *extra, bands[t])
        extra = ()
        by_mask[t] = swap_sub(msg, masks[t])
    gradient, field = call(functools.partial(finish_kernel, cfg), (shape(8, LANE), shape(24, nodes)))(
        own, dense, edge, *by_mask
    )
    return gradient, field.reshape(3, 8, nodes)


def solution(mesh):
    curves, subs = mesh.shape["curve"], mesh.shape["sub"]
    in_specs = (
        P(None, AX),
        P(None, AX),
        P(None, AX),
        P(None, None, AX),
        P(None, AX),
        P(AX),
        P(AX),
    )
    out_specs = (P(None, AX), P(None, None, AX))
    return jax.shard_map(
        functools.partial(local, curves, subs), mesh=mesh, in_specs=in_specs, out_specs=out_specs, check_vma=False
    )
```

```python
import functools

import jax
import jax.numpy as jnp
from jax import lax
from jax.experimental import pallas as pl
from jax.experimental.pallas import tpu as pltpu
from jax.sharding import PartitionSpec as P

BAND = 128
LANE = 128
WIDE = 256
AX = ("curve", "sub")
VMEM = pl.BlockSpec(memory_space=pltpu.VMEM)
SMEM = pl.BlockSpec(memory_space=pltpu.SMEM)
HBM = pl.BlockSpec(memory_space=pltpu.HBM)
f32 = jnp.float32


def params(mib):
    return pltpu.CompilerParams(vmem_limit_bytes=mib << 20)


def xor_order(subs):
    order, masks = [0], []
    while len(order) < subs:
        mask = 2 * len(order) - 1
        masks.append(mask)
        order = order + [mask ^ r for r in order]
    return order, masks


def fill(rest):
    rest, pairs = list(rest), []
    if len(rest) % 2:
        a, b, c = rest[-3:]
        rest = rest[:-3]
        pairs += [(a, b), (b, c), (c, a)]
    for i in range(0, len(rest), 2):
        pairs += [(rest[i], rest[i + 1]), (rest[i + 1], rest[i])]
    return pairs


def edge_pairs(curves, subs, place):
    pairs = []
    for g in range(curves):
        busy = set()
        if g > 0:
            busy.add(place)
        if g < curves - 1:
            busy.add(subs - 1)
            a, b = subs * g + subs - 1, subs * (g + 1) + place
            pairs += [(a, b), (b, a)]
        pairs += fill(subs * g + i for i in range(subs) if i not in busy)
    return pairs


def pack_kernel(direction, velocity, owner, out, velocity_out, owner_out, dirs, sems):
    copies = [
        pltpu.make_async_copy(direction, dirs, sems.at[0]),
        pltpu.make_async_copy(velocity, velocity_out, sems.at[1]),
        pltpu.make_async_copy(owner, owner_out, sems.at[2]),
    ]
    for c in copies:
        c.start()
    for c in copies:
        c.wait()
    out[0:8, :] = dirs[...]
    out[8:11, :] = velocity_out[:, :BAND]
    out[11:12, :] = owner_out[:, :BAND].astype(f32)
    out[12:16, :] = jnp.zeros((4, LANE), f32)


def prep_kernel(cfg, after, kmat, conn, weight, kmat_out, conn_out, weight_out, one_out, sems):
    subs, order, masks, nodes, basal, corners = cfg
    copies = [
        pltpu.make_async_copy(conn, conn_out, sems.at[0]),
        pltpu.make_async_copy(weight, weight_out, sems.at[1]),
        pltpu.make_async_copy(kmat, kmat_out, sems.at[2]),
    ]
    for c in copies:
        c.start()
    copies[0].wait()
    sub = lax.broadcasted_iota(jnp.int32, (WIDE, LANE), 0)
    for n in range(corners):
        row = conn_out[n : n + 1, :] - (nodes - BAND)
        low = jnp.broadcast_to(row & (WIDE - 1), (WIDE, LANE))
        one_out[:, n * LANE : (n + 1) * LANE] = (low == sub).astype(f32).astype(jnp.bfloat16)
    copies[1].wait()
    copies[2].wait()


def grow_kernel(held, got, out):
    dirs = held.shape[0] - 8
    out[0:dirs, :] = held[0:dirs, :]
    out[dirs : 2 * dirs, :] = got[0:dirs, :]
    out[2 * dirs : 2 * dirs + 8, :] = held[dirs : dirs + 8, :]


def rows8(row):
    return jnp.broadcast_to(row, (8, LANE))


def lanes_of(table, index):
    return jnp.take_along_axis(table, index, axis=1, mode="promise_in_bounds")


def lookup(owner_row, tables, shards):
    low = rows8(owner_row & (LANE - 1))
    high = rows8(owner_row >> 7)
    out = jnp.zeros((8, LANE), f32)
    for table, shard in zip(tables, shards):
        out = jnp.where(high == shard, lanes_of(table, low), out)
    return out


def gather_corners(field, blocks, conn, base, corners, v_ref):
    held = {(c, b): field(c, b) for c in range(3) for b in blocks}
    for n in range(corners):
        row = conn[n : n + 1, :] - base
        low = rows8(row & (LANE - 1))
        high = rows8(row >> 7)
        tests = {b: high == b for b in blocks}
        for c in range(3):
            acc = jnp.zeros((8, LANE), f32)
            for b in blocks:
                acc = jnp.where(tests[b], lanes_of(held[c, b], low), acc)
            v_ref[c * corners + n] = acc


def product(k_ref, v_ref, o_ref, size, group=9):
    count = size // group
    for i in range(size):
        o_ref[i] = jnp.zeros((8, LANE), f32)

    def step(block, carry):
        i0 = block * group
        vi = [v_ref[i0 + t] for t in range(group)]
        acc = [jnp.zeros((8, LANE), f32) for _ in range(group)]
        for t in range(group):
            for u in range(group):
                acc[t] = acc[t] + rows8(k_ref[i0 + t, pl.ds(i0 + u, 1), :]) * vi[u]
        for d in range(1, count // 2 + 1):
            j0 = jnp.where(block + d >= count, block + d - count, block + d) * group
            vj = [v_ref[j0 + u] for u in range(group)]
            far = [o_ref[j0 + u] for u in range(group)]
            for t in range(group):
                for u in range(group):
                    k = rows8(k_ref[i0 + t, pl.ds(j0 + u, 1), :])
                    acc[t] = acc[t] + k * vj[u]
                    far[u] = far[u] + k * vi[t]
            for u in range(group):
                o_ref[j0 + u] = far[u]
        for t in range(group):
            o_ref[i0 + t] += acc[t]
        return carry

    lax.fori_loop(0, count, step, 0)


def halves(x):
    high = x.astype(jnp.bfloat16).astype(f32)
    return high, x - high


def scatter_corners(o_ref, count, conn, base, corners, blocks, a_ref, one_ref):
    live = lax.broadcasted_iota(jnp.int32, (8, LANE), 1) < count
    wides = blocks * LANE // WIDE
    for n in range(corners):
        high = jnp.where(live, rows8((conn[n : n + 1, :] - base) >> 8), -1)
        parts = [halves(o_ref[c * corners + n]) for c in range(3)]
        stack = jnp.concatenate([p[0] for p in parts] + [p[1] for p in parts], axis=0).astype(jnp.bfloat16)
        for b in range(wides):
            here = (high == b).astype(f32).astype(jnp.bfloat16)
            a_ref[b * 48 : (b + 1) * 48, n * LANE : (n + 1) * LANE] = stack * jnp.concatenate([here] * 6, axis=0)
    res = lax.dot_general(
        a_ref[...], one_ref[...], (((1,), (1,)), ((), ())), preferred_element_type=f32
    )
    sums = []
    for b in range(wides):
        both = res[b * 48 : b * 48 + 24] + res[b * 48 + 24 : b * 48 + 48]
        sums += [both[:, h * LANE : (h + 1) * LANE] for h in range(WIDE // LANE)]
    return sums


def forward_kernel(cfg, *refs):
    subs, order, masks, nodes, basal, corners = cfg
    steps = len(masks)
    held, got, (low_b, mid_b) = refs[0], refs[1 : 1 + steps], refs[1 + steps : 3 + steps]
    velocity, owner, weight, kmat, conn, one_ref, count = refs[3 + steps : 10 + steps]
    ext, edge_out, info_out = refs[10 + steps : 13 + steps]
    swaps_out = refs[13 + steps : 13 + 2 * steps]
    v_ref, o_ref, a_ref = refs[13 + 2 * steps :]
    s = lax.axis_index("sub")
    half = subs // 2
    own_blocks = nodes // LANE
    blocks = own_blocks + 2
    last = s == subs - 1
    dirs = 8 * half

    info = low_b[dirs : dirs + 8, :]
    for t in range(steps):
        rows = got[t].shape[0]
        chain = (s & (2 * (1 << t) - 1)) == (1 << t) - 1
        info = jnp.where(chain, got[t][rows - 8 : rows, :], info)
    info = jnp.where(last, low_b[dirs : dirs + 8, :], info)
    info_out[...] = info

    mine = [held[8 * q : 8 * q + 8, :] for q in range(half)]
    mine += [got[-1][8 * q : 8 * q + 8, :] for q in range(half)]
    shards = [s ^ r for r in order]
    theirs = [low_b[8 * q : 8 * q + 8, :] for q in range(half)]
    theirs += [mid_b[8 * q : 8 * q + 8, :] for q in range(half)]
    their_shards = [order[q] for q in range(half)] + [half ^ order[q] for q in range(half)]
    next_tables = [jnp.where(last, b, a) for a, b in zip(mine, theirs)]
    next_shards = [jnp.where(last, b, a) for a, b in zip(shards, their_shards)]

    values = {}
    for b in range(basal // LANE):
        beta = lookup(owner[:, b * LANE : (b + 1) * LANE], mine, shards)
        for c in range(3):
            values[c, 1 + b] = rows8(velocity[c : c + 1, b * LANE : (b + 1) * LANE]) * beta
    beta = lookup(info[3:4, :].astype(jnp.int32), next_tables, next_shards)
    for c in range(3):
        values[c, blocks - 1] = rows8(info[c : c + 1, :]) * beta
    live_blocks = [1 + b for b in range(basal // LANE)] + [blocks - 1]
    base = nodes - BAND
    gather_corners(lambda c, b: values[c, b], live_blocks, conn, base, corners, v_ref)
    product(kmat, v_ref, o_ref, 3 * corners)
    sums = scatter_corners(o_ref, count[0], conn, base, corners, blocks, a_ref, one_ref)
    for b in range(blocks):
        ext[:, b * LANE : (b + 1) * LANE] = sums[b]
    pad = jnp.zeros((5, LANE), f32)
    none = jnp.zeros((8, LANE), f32)
    w_low = jnp.concatenate([weight[:, 0:BAND], pad], axis=0)
    w_high = jnp.concatenate([weight[:, nodes - BAND : nodes], pad], axis=0)
    before = ((sums[0], none), (sums[1], w_low))
    after = ((sums[blocks - 2], w_high), (sums[blocks - 1], none))
    for col in range(2):
        for part, rows in ((0, slice(0, 24)), (1, slice(24, 32))):
            down, up = before[col][part], after[col][part]
            lanes = slice(col * LANE, (col + 1) * LANE)
            for t in range(steps):
                swaps_out[t][rows, lanes] = jnp.where((s & (1 << t)) == 0, up, down)
            edge_out[rows, lanes] = jnp.where(last, up, jnp.where(s == 0, down, 0.0))


def neighbours(s, edge, swaps, subs):
    prev = nxt = edge
    for t, got in enumerate(swaps):
        ones = (1 << t) - 1
        nxt = jnp.where((s & (2 * ones + 1)) == ones, got, nxt)
        prev = jnp.where((s & (2 * ones + 1)) == ones + 1, got, prev)
    nxt = jnp.where(s == subs - 1, edge, nxt)
    return prev, nxt


def adjoint_kernel(cfg, *refs):
    subs, order, masks, nodes, basal, corners = cfg
    steps = len(masks)
    ext, edge_in, info, velocity, owner, weight, kmat, conn, one_ref, count = refs[:10]
    swaps_in = refs[10 : 10 + steps]
    n_out = 4 + steps
    outs = refs[10 + steps : 10 + steps + n_out]
    v_ref, o_ref, a_ref = refs[10 + steps + n_out :]
    own_out, swap_out, edge_out, mid_out = outs[:4]
    dense_out = outs[4]
    band_outs = outs[5:]
    s = lax.axis_index("sub")
    half = subs // 2
    blocks = nodes // LANE + 2
    last = s == subs - 1
    base = nodes - BAND
    prev, nxt = neighbours(s, edge_in[...], [x[...] for x in swaps_in], subs)

    values = {}
    for c in range(3):
        part = slice(8 * c, 8 * c + 8)
        for b in range(blocks):
            x = ext[part, b * LANE : (b + 1) * LANE]
            if b == 0:
                x = (x + prev[part, 0:LANE]) * rows8(prev[24 + c : 25 + c, 0:LANE])
            elif b == blocks - 1:
                x = (x + nxt[part, LANE:]) * rows8(nxt[24 + c : 25 + c, LANE:])
            else:
                if b == 1:
                    x = x + prev[part, LANE:]
                if b == blocks - 2:
                    x = x + nxt[part, 0:LANE]
                x = x * rows8(weight[c : c + 1, (b - 1) * LANE : b * LANE])
            values[c, b] = x
    gather_corners(lambda c, b: values[c, b], range(blocks), conn, base, corners, v_ref)
    product(kmat, v_ref, o_ref, 3 * corners)
    sums = scatter_corners(o_ref, count[0], conn, base, corners, blocks, a_ref, one_ref)
    for b in range(1, blocks - 1):
        own_out[:, (b - 1) * LANE : b * LANE] = sums[b]
    lower, upper = sums[0], sums[blocks - 1]

    n_basal = basal // LANE
    terms, owners = [], []
    for b in range(n_basal):
        terms.append(
            sum(
                rows8(velocity[c : c + 1, b * LANE : (b + 1) * LANE]) * sums[1 + b][8 * c : 8 * c + 8]
                for c in range(3)
            )
        )
        owners.append(owner[:, b * LANE : (b + 1) * LANE])
    beyond = sum(rows8(info[c : c + 1, :]) * upper[8 * c : 8 * c + 8] for c in range(3))
    terms.append(jnp.where(last, 0.0, beyond))
    owners.append(info[3:4, :].astype(jnp.int32))
    across = jnp.where(last, beyond, 0.0)
    sub_iota = lax.broadcasted_iota(jnp.int32, (LANE, LANE), 0)
    one = jnp.concatenate(
        [
            (jnp.broadcast_to(o & (LANE - 1), (LANE, LANE)) == sub_iota).astype(f32).astype(jnp.bfloat16)
            for o in owners
        ],
        axis=1,
    )
    split = [halves(t) for t in terms]
    split_across = halves(across)
    zero = jnp.zeros((8, LANE), f32)
    lines = []
    for r in order:
        here = [rows8(o >> 7) == (s ^ r) for o in owners]
        for piece in range(2):
            lines.append(
                jnp.concatenate([jnp.where(h, t[piece], 0.0) for h, t in zip(here, split)], axis=1)
            )
    for q in range(subs):
        shard = order[q] if q < half else half ^ order[q - half]
        here = rows8(owners[-1] >> 7) == shard
        for piece in range(2):
            lines.append(
                jnp.concatenate(
                    [zero] * n_basal + [jnp.where(here, split_across[piece], 0.0)], axis=1
                )
            )
    res = lax.dot_general(
        jnp.concatenate(lines, axis=0).astype(jnp.bfloat16),
        one,
        (((1,), (1,)), ((), ())),
        preferred_element_type=f32,
    )
    dense = [res[16 * q : 16 * q + 8] + res[16 * q + 8 : 16 * q + 16] for q in range(2 * subs)]
    rows = 8 * half
    for q in range(half):
        dense_out[8 * q : 8 * q + 8, :] = dense[q]
        swap_out[8 * q : 8 * q + 8, :] = dense[half + q]
        edge_out[8 * q : 8 * q + 8, :] = dense[subs + q]
        mid_out[8 * q : 8 * q + 8, :] = dense[subs + half + q]
    edge_out[rows : rows + 24, :] = jnp.where(last, upper, jnp.where(s == 0, lower, 0.0))
    up = (s & half) == 0
    swap_out[rows : rows + 24, :] = jnp.where(up, upper, lower)
    for t, band in enumerate(band_outs):
        up = (s & (1 << t)) == 0
        band[...] = jnp.where(up, upper, lower)


def shrink_kernel(first, *refs):
    if first:
        held, got, edge, mid, band, msg, left = refs
    else:
        held, got, band, msg, left = refs
    rows = held.shape[0]
    total = held[...] + got[0:rows, :]
    if first:
        total = total + edge[0:rows, :] + mid[...]
    keep = rows // 2
    left[...] = total[0:keep]
    msg[0:keep, :] = total[keep:]
    msg[keep : keep + 24, :] = band[...]


def finish_kernel(cfg, *refs):
    subs, order, masks, nodes, basal, corners = cfg
    steps = len(masks)
    own, held, edge = refs[:3]
    got = refs[3 : 3 + steps]
    gradient, field = refs[3 + steps :]
    s = lax.axis_index("sub")
    gradient[...] = held[...] + got[0][0:8, :]
    bands = [g[g.shape[0] - 24 :, :] for g in got]
    prev, nxt = neighbours(s, edge[edge.shape[0] - 24 :, :], bands, subs)
    field[:, 0:LANE] = own[:, 0:LANE] + prev
    field[:, LANE : nodes - LANE] = own[:, LANE : nodes - LANE]
    field[:, nodes - LANE :] = own[:, nodes - LANE :] + nxt


def shape(*dims):
    return jax.ShapeDtypeStruct(dims, f32)


def local(curves, subs, direction, base_velocity, weight, element_matrix, connectivity, element_count, basal_owner):
    order, masks = xor_order(subs)
    half = subs // 2
    nodes = base_velocity.shape[1]
    basal = basal_owner.shape[0]
    corners, elems = connectivity.shape
    size = 3 * corners
    blocks = nodes // LANE + 2
    cfg = (subs, order, masks, nodes, basal, corners)
    owner = basal_owner.reshape(1, basal)

    def call(kernel, out_shape, scratch=(), mib=4, specs=None, cost=None):
        def run(*args):
            return pl.pallas_call(
                kernel,
                out_shape=out_shape,
                in_specs=specs or [VMEM] * len(args),
                out_specs=jax.tree.map(lambda _: VMEM, out_shape),
                scratch_shapes=list(scratch),
                compiler_params=params(mib),
                cost_estimate=cost,
            )(*args)

        return run

    def swap_sub(x, mask):
        return lax.ppermute(x, "sub", [(i, i ^ mask) for i in range(subs)])

    def swap_edge(x, place):
        return lax.ppermute(x, AX, edge_pairs(curves, subs, place))

    steps = len(masks)
    rows = 8 * half

    held, velocity, owner = call(
        pack_kernel,
        (shape(16, LANE), shape(3, nodes), jax.ShapeDtypeStruct((1, basal), jnp.int32)),
        [pltpu.VMEM((8, LANE), f32), pltpu.SemaphoreType.DMA((3,))],
        specs=[HBM] * 3,
    )(direction, base_velocity, owner)
    got = []
    for mask in masks[:-1]:
        got.append(swap_sub(held, mask))
        held = call(grow_kernel, shape(2 * held.shape[0] - 8, LANE))(held, got[-1])
    low_b = swap_edge(held, 0)
    mid_b = swap_edge(held, half)
    got.append(swap_sub(held, masks[-1]))

    kmat, conn, weight, one = call(
        functools.partial(prep_kernel, cfg),
        (
            shape(size, size, elems),
            jax.ShapeDtypeStruct((corners, elems), jnp.int32),
            shape(3, nodes),
            jax.ShapeDtypeStruct((WIDE, corners * LANE), jnp.bfloat16),
        ),
        [pltpu.SemaphoreType.DMA((3,))],
        16,
        [VMEM] + [HBM] * 3,
        pl.CostEstimate(flops=0, bytes_accessed=8 << 20, transcendentals=0),
    )(held, element_matrix, connectivity, weight)

    scratch = [
        pltpu.VMEM((size, 8, LANE), f32),
        pltpu.VMEM((size, 8, LANE), f32),
        pltpu.VMEM((48 * blocks * LANE // WIDE, corners * LANE), jnp.bfloat16),
    ]
    ext, edge, info, *swaps = call(
        functools.partial(forward_kernel, cfg),
        (shape(24, blocks * LANE), shape(32, 2 * LANE), shape(8, LANE)) + (shape(32, 2 * LANE),) * steps,
        scratch,
        16,
        [VMEM] * (9 + steps) + [SMEM],
    )(held, *got, low_b, mid_b, velocity, owner, weight, kmat, conn, one, element_count)

    edge = swap_edge(edge, 0)
    swaps = [swap_sub(x, mask) for x, mask in zip(swaps, masks)]

    own, swap_msg, edge_msg, mid_msg, dense, *bands = call(
        functools.partial(adjoint_kernel, cfg),
        (shape(24, nodes), shape(rows + 24, LANE), shape(rows + 24, LANE), shape(rows, LANE), shape(rows, LANE))
        + (shape(24, LANE),) * (steps - 1),
        scratch,
        16,
        [VMEM] * 9 + [SMEM] + [VMEM] * steps,
    )(ext, edge, info, velocity, owner, weight, kmat, conn, one, element_count, *swaps)

    edge = swap_edge(edge_msg, 0)
    mid = swap_edge(mid_msg, half)
    by_mask = [None] * steps
    by_mask[-1] = swap_sub(swap_msg, masks[-1])
    extra = (edge, mid)
    for t in range(steps - 2, -1, -1):
        keep = dense.shape[0] // 2
        msg, dense = call(
            functools.partial(shrink_kernel, bool(extra)), (shape(keep + 24, LANE), shape(keep, LANE))
        )(dense, by_mask[t + 1], *extra, bands[t])
        extra = ()
        by_mask[t] = swap_sub(msg, masks[t])
    gradient, field = call(functools.partial(finish_kernel, cfg), (shape(8, LANE), shape(24, nodes)))(
        own, dense, edge, *by_mask
    )
    return gradient, field.reshape(3, 8, nodes)


def solution(mesh):
    curves, subs = mesh.shape["curve"], mesh.shape["sub"]
    in_specs = (
        P(None, AX),
        P(None, AX),
        P(None, AX),
        P(None, None, AX),
        P(None, AX),
        P(AX),
        P(AX),
    )
    out_specs = (P(None, AX), P(None, None, AX))
    return jax.shard_map(
        functools.partial(local, curves, subs), mesh=mesh, in_specs=in_specs, out_specs=out_specs, check_vma=False
    )
```

```python
import functools

import jax
import jax.numpy as jnp
from jax import lax
from jax.experimental import pallas as pl
from jax.experimental.pallas import tpu as pltpu
from jax.sharding import PartitionSpec as P

BAND = 128
LANE = 128
WIDE = 256
AX = ("curve", "sub")
VMEM = pl.BlockSpec(memory_space=pltpu.VMEM)
SMEM = pl.BlockSpec(memory_space=pltpu.SMEM)
HBM = pl.BlockSpec(memory_space=pltpu.HBM)
f32 = jnp.float32


def params(mib):
    return pltpu.CompilerParams(vmem_limit_bytes=mib << 20)


def xor_order(subs):
    order, masks = [0], []
    while len(order) < subs:
        mask = 2 * len(order) - 1
        masks.append(mask)
        order = order + [mask ^ r for r in order]
    return order, masks


def fill(rest):
    rest, pairs = list(rest), []
    if len(rest) % 2:
        a, b, c = rest[-3:]
        rest = rest[:-3]
        pairs += [(a, b), (b, c), (c, a)]
    for i in range(0, len(rest), 2):
        pairs += [(rest[i], rest[i + 1]), (rest[i + 1], rest[i])]
    return pairs


def edge_pairs(curves, subs, place):
    pairs = []
    for g in range(curves):
        busy = set()
        if g > 0:
            busy.add(place)
        if g < curves - 1:
            busy.add(subs - 1)
            a, b = subs * g + subs - 1, subs * (g + 1) + place
            pairs += [(a, b), (b, a)]
        pairs += fill(subs * g + i for i in range(subs) if i not in busy)
    return pairs


def pack_kernel(direction, velocity, owner, out, velocity_out, owner_out, dirs, sems):
    copies = [
        pltpu.make_async_copy(direction, dirs, sems.at[0]),
        pltpu.make_async_copy(velocity, velocity_out, sems.at[1]),
        pltpu.make_async_copy(owner, owner_out, sems.at[2]),
    ]
    for c in copies:
        c.start()
    for c in copies:
        c.wait()
    out[0:8, :] = dirs[...]
    out[8:11, :] = velocity_out[:, :BAND]
    out[11:12, :] = owner_out[:, :BAND].astype(f32)
    out[12:16, :] = jnp.zeros((4, LANE), f32)


def prep_kernel(cfg, after, kmat, conn, weight, kmat_out, conn_out, weight_out, one_out, sems):
    subs, order, masks, nodes, basal, corners = cfg
    copies = [
        pltpu.make_async_copy(conn, conn_out, sems.at[0]),
        pltpu.make_async_copy(weight, weight_out, sems.at[1]),
        pltpu.make_async_copy(kmat, kmat_out, sems.at[2]),
    ]
    for c in copies:
        c.start()
    copies[0].wait()
    sub = lax.broadcasted_iota(jnp.int32, (WIDE, LANE), 0)
    for n in range(corners):
        row = conn_out[n : n + 1, :] - (nodes - BAND)
        low = jnp.broadcast_to(row & (WIDE - 1), (WIDE, LANE))
        one_out[:, n * LANE : (n + 1) * LANE] = (low == sub).astype(f32).astype(jnp.bfloat16)
    copies[1].wait()
    copies[2].wait()


def grow_kernel(held, got, out):
    dirs = held.shape[0] - 8
    out[0:dirs, :] = held[0:dirs, :]
    out[dirs : 2 * dirs, :] = got[0:dirs, :]
    out[2 * dirs : 2 * dirs + 8, :] = held[dirs : dirs + 8, :]


def rows8(row):
    return jnp.broadcast_to(row, (8, LANE))


def lanes_of(table, index):
    return jnp.take_along_axis(table, index, axis=1, mode="promise_in_bounds")


def lookup(owner_row, tables, shards):
    low = rows8(owner_row & (LANE - 1))
    high = rows8(owner_row >> 7)
    out = jnp.zeros((8, LANE), f32)
    for table, shard in zip(tables, shards):
        out = jnp.where(high == shard, lanes_of(table, low), out)
    return out


def gather_corners(field, blocks, conn, base, corners, v_ref):
    held = {(c, b): field(c, b) for c in range(3) for b in blocks}
    for n in range(corners):
        row = conn[n : n + 1, :] - base
        low = rows8(row & (LANE - 1))
        high = rows8(row >> 7)
        tests = {b: high == b for b in blocks}
        for c in range(3):
            acc = jnp.zeros((8, LANE), f32)
            for b in blocks:
                acc = jnp.where(tests[b], lanes_of(held[c, b], low), acc)
            v_ref[c * corners + n] = acc


def product(k_ref, v_ref, o_ref, size, group=9):
    count = size // group
    for i in range(size):
        o_ref[i] = jnp.zeros((8, LANE), f32)

    def step(block, carry):
        i0 = block * group
        vi = [v_ref[i0 + t] for t in range(group)]
        acc = [jnp.zeros((8, LANE), f32) for _ in range(group)]
        for t in range(group):
            for u in range(group):
                acc[t] = acc[t] + rows8(k_ref[i0 + t, pl.ds(i0 + u, 1), :]) * vi[u]
        for d in range(1, count // 2 + 1):
            j0 = jnp.where(block + d >= count, block + d - count, block + d) * group
            vj = [v_ref[j0 + u] for u in range(group)]
            far = [o_ref[j0 + u] for u in range(group)]
            for t in range(group):
                for u in range(group):
                    k = rows8(k_ref[i0 + t, pl.ds(j0 + u, 1), :])
                    acc[t] = acc[t] + k * vj[u]
                    far[u] = far[u] + k * vi[t]
            for u in range(group):
                o_ref[j0 + u] = far[u]
        for t in range(group):
            o_ref[i0 + t] += acc[t]
        return carry

    lax.fori_loop(0, count, step, 0)


def halves(x):
    high = x.astype(jnp.bfloat16).astype(f32)
    return high, x - high


def scatter_corners(o_ref, count, conn, base, corners, blocks, a_ref, one_ref):
    live = lax.broadcasted_iota(jnp.int32, (8, LANE), 1) < count
    wides = blocks * LANE // WIDE
    for n in range(corners):
        high = jnp.where(live, rows8((conn[n : n + 1, :] - base) >> 8), -1)
        parts = [halves(o_ref[c * corners + n]) for c in range(3)]
        stack = jnp.concatenate([p[0] for p in parts] + [p[1] for p in parts], axis=0).astype(jnp.bfloat16)
        for b in range(wides):
            here = (high == b).astype(f32).astype(jnp.bfloat16)
            a_ref[b * 48 : (b + 1) * 48, n * LANE : (n + 1) * LANE] = stack * jnp.concatenate([here] * 6, axis=0)
    res = lax.dot_general(
        a_ref[...], one_ref[...], (((1,), (1,)), ((), ())), preferred_element_type=f32
    )
    sums = []
    for b in range(wides):
        both = res[b * 48 : b * 48 + 24] + res[b * 48 + 24 : b * 48 + 48]
        sums += [both[:, h * LANE : (h + 1) * LANE] for h in range(WIDE // LANE)]
    return sums


def forward_kernel(cfg, *refs):
    subs, order, masks, nodes, basal, corners = cfg
    steps = len(masks)
    held, got, (low_b, mid_b) = refs[0], refs[1 : 1 + steps], refs[1 + steps : 3 + steps]
    velocity, owner, weight, kmat, conn, one_ref, count = refs[3 + steps : 10 + steps]
    ext, edge_out, info_out = refs[10 + steps : 13 + steps]
    swaps_out = refs[13 + steps : 13 + 2 * steps]
    v_ref, o_ref, a_ref = refs[13 + 2 * steps :]
    s = lax.axis_index("sub")
    half = subs // 2
    own_blocks = nodes // LANE
    blocks = own_blocks + 2
    last = s == subs - 1
    dirs = 8 * half

    info = low_b[dirs : dirs + 8, :]
    for t in range(steps):
        rows = got[t].shape[0]
        chain = (s & (2 * (1 << t) - 1)) == (1 << t) - 1
        info = jnp.where(chain, got[t][rows - 8 : rows, :], info)
    info = jnp.where(last, low_b[dirs : dirs + 8, :], info)
    info_out[...] = info

    mine = [held[8 * q : 8 * q + 8, :] for q in range(half)]
    mine += [got[-1][8 * q : 8 * q + 8, :] for q in range(half)]
    shards = [s ^ r for r in order]
    theirs = [low_b[8 * q : 8 * q + 8, :] for q in range(half)]
    theirs += [mid_b[8 * q : 8 * q + 8, :] for q in range(half)]
    their_shards = [order[q] for q in range(half)] + [half ^ order[q] for q in range(half)]
    next_tables = [jnp.where(last, b, a) for a, b in zip(mine, theirs)]
    next_shards = [jnp.where(last, b, a) for a, b in zip(shards, their_shards)]

    values = {}
    for b in range(basal // LANE):
        beta = lookup(owner[:, b * LANE : (b + 1) * LANE], mine, shards)
        for c in range(3):
            values[c, 1 + b] = rows8(velocity[c : c + 1, b * LANE : (b + 1) * LANE]) * beta
    beta = lookup(info[3:4, :].astype(jnp.int32), next_tables, next_shards)
    for c in range(3):
        values[c, blocks - 1] = rows8(info[c : c + 1, :]) * beta
    live_blocks = [1 + b for b in range(basal // LANE)] + [blocks - 1]
    base = nodes - BAND
    gather_corners(lambda c, b: values[c, b], live_blocks, conn, base, corners, v_ref)
    product(kmat, v_ref, o_ref, 3 * corners)
    sums = scatter_corners(o_ref, count[0], conn, base, corners, blocks, a_ref, one_ref)
    for b in range(blocks):
        ext[:, b * LANE : (b + 1) * LANE] = sums[b]
    pad = jnp.zeros((5, LANE), f32)
    none = jnp.zeros((8, LANE), f32)
    w_low = jnp.concatenate([weight[:, 0:BAND], pad], axis=0)
    w_high = jnp.concatenate([weight[:, nodes - BAND : nodes], pad], axis=0)
    before = ((sums[0], none), (sums[1], w_low))
    after = ((sums[blocks - 2], w_high), (sums[blocks - 1], none))
    for col in range(2):
        for part, rows in ((0, slice(0, 24)), (1, slice(24, 32))):
            down, up = before[col][part], after[col][part]
            lanes = slice(col * LANE, (col + 1) * LANE)
            for t in range(steps):
                swaps_out[t][rows, lanes] = jnp.where((s & (1 << t)) == 0, up, down)
            edge_out[rows, lanes] = jnp.where(last, up, jnp.where(s == 0, down, 0.0))


def neighbours(s, edge, swaps, subs):
    prev = nxt = edge
    for t, got in enumerate(swaps):
        ones = (1 << t) - 1
        nxt = jnp.where((s & (2 * ones + 1)) == ones, got, nxt)
        prev = jnp.where((s & (2 * ones + 1)) == ones + 1, got, prev)
    nxt = jnp.where(s == subs - 1, edge, nxt)
    return prev, nxt


def adjoint_kernel(cfg, *refs):
    subs, order, masks, nodes, basal, corners = cfg
    steps = len(masks)
    ext, edge_in, info, velocity, owner, weight, kmat, conn, one_ref, count = refs[:10]
    swaps_in = refs[10 : 10 + steps]
    n_out = 4 + steps
    outs = refs[10 + steps : 10 + steps + n_out]
    v_ref, o_ref, a_ref = refs[10 + steps + n_out :]
    own_out, swap_out, edge_out, mid_out = outs[:4]
    dense_out = outs[4]
    band_outs = outs[5:]
    s = lax.axis_index("sub")
    half = subs // 2
    blocks = nodes // LANE + 2
    last = s == subs - 1
    base = nodes - BAND
    prev, nxt = neighbours(s, edge_in[...], [x[...] for x in swaps_in], subs)

    values = {}
    for c in range(3):
        part = slice(8 * c, 8 * c + 8)
        for b in range(blocks):
            x = ext[part, b * LANE : (b + 1) * LANE]
            if b == 0:
                x = (x + prev[part, 0:LANE]) * rows8(prev[24 + c : 25 + c, 0:LANE])
            elif b == blocks - 1:
                x = (x + nxt[part, LANE:]) * rows8(nxt[24 + c : 25 + c, LANE:])
            else:
                if b == 1:
                    x = x + prev[part, LANE:]
                if b == blocks - 2:
                    x = x + nxt[part, 0:LANE]
                x = x * rows8(weight[c : c + 1, (b - 1) * LANE : b * LANE])
            values[c, b] = x
    gather_corners(lambda c, b: values[c, b], range(blocks), conn, base, corners, v_ref)
    product(kmat, v_ref, o_ref, 3 * corners)
    sums = scatter_corners(o_ref, count[0], conn, base, corners, blocks, a_ref, one_ref)
    for b in range(1, blocks - 1):
        own_out[:, (b - 1) * LANE : b * LANE] = sums[b]
    lower, upper = sums[0], sums[blocks - 1]

    n_basal = basal // LANE
    terms, owners = [], []
    for b in range(n_basal):
        terms.append(
            sum(
                rows8(velocity[c : c + 1, b * LANE : (b + 1) * LANE]) * sums[1 + b][8 * c : 8 * c + 8]
                for c in range(3)
            )
        )
        owners.append(owner[:, b * LANE : (b + 1) * LANE])
    beyond = sum(rows8(info[c : c + 1, :]) * upper[8 * c : 8 * c + 8] for c in range(3))
    terms.append(jnp.where(last, 0.0, beyond))
    owners.append(info[3:4, :].astype(jnp.int32))
    across = jnp.where(last, beyond, 0.0)
    sub_iota = lax.broadcasted_iota(jnp.int32, (LANE, LANE), 0)
    one = jnp.concatenate(
        [
            (jnp.broadcast_to(o & (LANE - 1), (LANE, LANE)) == sub_iota).astype(f32).astype(jnp.bfloat16)
            for o in owners
        ],
        axis=1,
    )
    split = [halves(t) for t in terms]
    split_across = halves(across)
    zero = jnp.zeros((8, LANE), f32)
    lines = []
    for r in order:
        here = [rows8(o >> 7) == (s ^ r) for o in owners]
        for piece in range(2):
            lines.append(
                jnp.concatenate([jnp.where(h, t[piece], 0.0) for h, t in zip(here, split)], axis=1)
            )
    for q in range(subs):
        shard = order[q] if q < half else half ^ order[q - half]
        here = rows8(owners[-1] >> 7) == shard
        for piece in range(2):
            lines.append(
                jnp.concatenate(
                    [zero] * n_basal + [jnp.where(here, split_across[piece], 0.0)], axis=1
                )
            )
    res = lax.dot_general(
        jnp.concatenate(lines, axis=0).astype(jnp.bfloat16),
        one,
        (((1,), (1,)), ((), ())),
        preferred_element_type=f32,
    )
    dense = [res[16 * q : 16 * q + 8] + res[16 * q + 8 : 16 * q + 16] for q in range(2 * subs)]
    rows = 8 * half
    for q in range(half):
        dense_out[8 * q : 8 * q + 8, :] = dense[q]
        swap_out[8 * q : 8 * q + 8, :] = dense[half + q]
        edge_out[8 * q : 8 * q + 8, :] = dense[subs + q]
        mid_out[8 * q : 8 * q + 8, :] = dense[subs + half + q]
    edge_out[rows : rows + 24, :] = jnp.where(last, upper, jnp.where(s == 0, lower, 0.0))
    up = (s & half) == 0
    swap_out[rows : rows + 24, :] = jnp.where(up, upper, lower)
    for t, band in enumerate(band_outs):
        up = (s & (1 << t)) == 0
        band[...] = jnp.where(up, upper, lower)


def shrink_kernel(first, *refs):
    if first:
        held, got, edge, mid, band, msg, left = refs
    else:
        held, got, band, msg, left = refs
    rows = held.shape[0]
    total = held[...] + got[0:rows, :]
    if first:
        total = total + edge[0:rows, :] + mid[...]
    keep = rows // 2
    left[...] = total[0:keep]
    msg[0:keep, :] = total[keep:]
    msg[keep : keep + 24, :] = band[...]


def finish_kernel(cfg, *refs):
    subs, order, masks, nodes, basal, corners = cfg
    steps = len(masks)
    own, held, edge = refs[:3]
    got = refs[3 : 3 + steps]
    gradient, field = refs[3 + steps :]
    s = lax.axis_index("sub")
    gradient[...] = held[...] + got[0][0:8, :]
    bands = [g[g.shape[0] - 24 :, :] for g in got]
    prev, nxt = neighbours(s, edge[edge.shape[0] - 24 :, :], bands, subs)
    field[:, 0:LANE] = own[:, 0:LANE] + prev
    field[:, LANE : nodes - LANE] = own[:, LANE : nodes - LANE]
    field[:, nodes - LANE :] = own[:, nodes - LANE :] + nxt


def shape(*dims):
    return jax.ShapeDtypeStruct(dims, f32)


def local(curves, subs, direction, base_velocity, weight, element_matrix, connectivity, element_count, basal_owner):
    order, masks = xor_order(subs)
    half = subs // 2
    nodes = base_velocity.shape[1]
    basal = basal_owner.shape[0]
    corners, elems = connectivity.shape
    size = 3 * corners
    blocks = nodes // LANE + 2
    cfg = (subs, order, masks, nodes, basal, corners)
    owner = basal_owner.reshape(1, basal)

    def call(kernel, out_shape, scratch=(), mib=4, specs=None, cost=None):
        def run(*args):
            args = [
                pltpu.with_memory_space_constraint(x, pltpu.HBM) if specs and specs[i] is HBM else x
                for i, x in enumerate(args)
            ]
            return pl.pallas_call(
                kernel,
                out_shape=out_shape,
                in_specs=specs or [VMEM] * len(args),
                out_specs=jax.tree.map(lambda _: VMEM, out_shape),
                scratch_shapes=list(scratch),
                compiler_params=params(mib),
                cost_estimate=cost,
            )(*args)

        return run

    def swap_sub(x, mask):
        return lax.ppermute(x, "sub", [(i, i ^ mask) for i in range(subs)])

    def swap_edge(x, place):
        return lax.ppermute(x, AX, edge_pairs(curves, subs, place))

    steps = len(masks)
    rows = 8 * half

    held, velocity, owner = call(
        pack_kernel,
        (shape(16, LANE), shape(3, nodes), jax.ShapeDtypeStruct((1, basal), jnp.int32)),
        [pltpu.VMEM((8, LANE), f32), pltpu.SemaphoreType.DMA((3,))],
        specs=[HBM] * 3,
    )(direction, base_velocity, owner)
    got = []
    for mask in masks[:-1]:
        got.append(swap_sub(held, mask))
        held = call(grow_kernel, shape(2 * held.shape[0] - 8, LANE))(held, got[-1])
    low_b = swap_edge(held, 0)
    mid_b = swap_edge(held, half)
    got.append(swap_sub(held, masks[-1]))

    kmat, conn, weight, one = call(
        functools.partial(prep_kernel, cfg),
        (
            shape(size, size, elems),
            jax.ShapeDtypeStruct((corners, elems), jnp.int32),
            shape(3, nodes),
            jax.ShapeDtypeStruct((WIDE, corners * LANE), jnp.bfloat16),
        ),
        [pltpu.SemaphoreType.DMA((3,))],
        16,
        [VMEM] + [HBM] * 3,
        pl.CostEstimate(flops=0, bytes_accessed=8 << 20, transcendentals=0),
    )(held, element_matrix, connectivity, weight)

    scratch = [
        pltpu.VMEM((size, 8, LANE), f32),
        pltpu.VMEM((size, 8, LANE), f32),
        pltpu.VMEM((48 * blocks * LANE // WIDE, corners * LANE), jnp.bfloat16),
    ]
    ext, edge, info, *swaps = call(
        functools.partial(forward_kernel, cfg),
        (shape(24, blocks * LANE), shape(32, 2 * LANE), shape(8, LANE)) + (shape(32, 2 * LANE),) * steps,
        scratch,
        16,
        [VMEM] * (9 + steps) + [SMEM],
    )(held, *got, low_b, mid_b, velocity, owner, weight, kmat, conn, one, element_count)

    edge = swap_edge(edge, 0)
    swaps = [swap_sub(x, mask) for x, mask in zip(swaps, masks)]

    own, swap_msg, edge_msg, mid_msg, dense, *bands = call(
        functools.partial(adjoint_kernel, cfg),
        (shape(24, nodes), shape(rows + 24, LANE), shape(rows + 24, LANE), shape(rows, LANE), shape(rows, LANE))
        + (shape(24, LANE),) * (steps - 1),
        scratch,
        16,
        [VMEM] * 9 + [SMEM] + [VMEM] * steps,
    )(ext, edge, info, velocity, owner, weight, kmat, conn, one, element_count, *swaps)

    edge = swap_edge(edge_msg, 0)
    mid = swap_edge(mid_msg, half)
    by_mask = [None] * steps
    by_mask[-1] = swap_sub(swap_msg, masks[-1])
    extra = (edge, mid)
    for t in range(steps - 2, -1, -1):
        keep = dense.shape[0] // 2
        msg, dense = call(
            functools.partial(shrink_kernel, bool(extra)), (shape(keep + 24, LANE), shape(keep, LANE))
        )(dense, by_mask[t + 1], *extra, bands[t])
        extra = ()
        by_mask[t] = swap_sub(msg, masks[t])
    gradient, field = call(functools.partial(finish_kernel, cfg), (shape(8, LANE), shape(24, nodes)))(
        own, dense, edge, *by_mask
    )
    return gradient, field.reshape(3, 8, nodes)


def solution(mesh):
    curves, subs = mesh.shape["curve"], mesh.shape["sub"]
    in_specs = (
        P(None, AX),
        P(None, AX),
        P(None, AX),
        P(None, None, AX),
        P(None, AX),
        P(AX),
        P(AX),
    )
    out_specs = (P(None, AX), P(None, None, AX))
    return jax.shard_map(
        functools.partial(local, curves, subs), mesh=mesh, in_specs=in_specs, out_specs=out_specs, check_vma=False
    )
```

```python
import functools

import jax
import jax.numpy as jnp
from jax import lax
from jax.experimental import pallas as pl
from jax.experimental.pallas import tpu as pltpu
from jax.sharding import PartitionSpec as P


BAND = 128
LANE = 128
WIDE = 256
GROUP = 9
ADJOINT_MATMUL = 16
EARLY = 5
AX = ("curve", "sub")
VMEM = pl.BlockSpec(memory_space=pltpu.VMEM)
SMEM = pl.BlockSpec(memory_space=pltpu.SMEM)
HBM = pl.BlockSpec(memory_space=pltpu.HBM)
f32 = jnp.float32


def params(mib):
    return pltpu.CompilerParams(vmem_limit_bytes=mib << 20)


def xor_order(subs):
    order, masks = [0], []
    while len(order) < subs:
        mask = 2 * len(order) - 1
        masks.append(mask)
        order = order + [mask ^ r for r in order]
    return order, masks


def fill(rest):
    rest, pairs = list(rest), []
    if len(rest) % 2:
        a, b, c = rest[-3:]
        rest = rest[:-3]
        pairs += [(a, b), (b, c), (c, a)]
    for i in range(0, len(rest), 2):
        pairs += [(rest[i], rest[i + 1]), (rest[i + 1], rest[i])]
    return pairs


def edge_pairs(curves, subs, place):
    pairs = []
    for g in range(curves):
        busy = set()
        if g > 0:
            busy.add(place)
        if g < curves - 1:
            busy.add(subs - 1)
            a, b = subs * g + subs - 1, subs * (g + 1) + place
            pairs += [(a, b), (b, a)]
        pairs += fill(subs * g + i for i in range(subs) if i not in busy)
    return pairs


def edge_swap(curves, subs, flip=False):
    half, pairs = subs // 2, []
    for g in range(curves):
        first = subs * g
        last, a, b = first + subs - 1, first + half - 1, first + half
        if g < curves - 1:
            pairs += [(last, last + 1), (last + 1, last)]
        if g == 0:
            cycle = (first, b, a)
        elif g == curves - 1:
            cycle = (a, b, last)
        else:
            cycle = (a, b)
        if flip:
            cycle = cycle[::-1]
        pairs += list(zip(cycle, cycle[1:] + cycle[:1]))
        for i in range(1, half - 1):
            pairs += [(first + i, last - i), (last - i, first + i)]
    return pairs


def ends_swap(curves, subs):
    pairs = []
    for g in range(curves):
        for i in range(subs):
            pairs.append((subs * g + i, subs * g + (subs - 1 - i if g in (0, curves - 1) else i ^ 1)))
    return pairs


def inner_swap(curves, subs, flip=False):
    half, pairs = subs // 2, []
    for g in range(curves):
        first = subs * g
        last, a, b = first + subs - 1, first + half - 1, first + half
        pairs += [(first, last), (last, first)]
        if g == 0:
            pairs.append((a, b))
        pairs.append((b, b + subs) if g < curves - 1 else (b, a))
        if g > 0:
            pairs.append((a, a - subs))
        pairs += fill(first + i for i in range(1, subs - 1) if i not in (half - 1, half))
    return [(b, a) for a, b in pairs] if flip else pairs


def pack_kernel(direction, velocity, owner, conn, weight, dirs, info, velocity_out, owner_out, conn_out, weight_out, sems):
    pairs = ((direction, dirs), (velocity, velocity_out), (owner, owner_out), (conn, conn_out), (weight, weight_out))
    copies = [pltpu.make_async_copy(a, b, sems.at[i]) for i, (a, b) in enumerate(pairs)]
    for c in copies:
        c.start()
    for c in copies:
        c.wait()
    info[0:3, :] = velocity_out[:, :BAND]
    info[3:4, :] = owner_out[:, :BAND].astype(f32)
    info[4:8, :] = jnp.zeros((4, LANE), f32)


def prep_kernel(cfg, after, kmat, conn, count, kmat_out, one_out, live_out, sems):
    _, _, _, nodes, _, corners, _ = cfg
    part = slice(0, EARLY * GROUP)
    early = pltpu.make_async_copy(kmat.at[part], kmat_out.at[part], sems.at[0])
    early.start()
    live = lax.broadcasted_iota(jnp.int32, (8, LANE), 1) < count[0]
    live_out[...] = live.astype(jnp.int32)
    sub = lax.broadcasted_iota(jnp.int32, (WIDE, LANE), 0)
    for first in range(0, corners, 2):
        some = range(first, min(first + 2, corners))
        hits = []
        for n in some:
            row = conn[n : n + 1, :] - (nodes - BAND)
            hits.append((jnp.broadcast_to(row & (WIDE - 1), (WIDE, LANE)) == sub).astype(f32))
        one_out[:, first * LANE : (first + len(some)) * LANE] = jnp.concatenate(hits, axis=1).astype(jnp.bfloat16)
    early.wait()


def grow_kernel(info, held, got, out):
    dirs = held.shape[0]
    out[0:dirs, :] = held[...]
    out[dirs : 2 * dirs, :] = got[...]
    if info is not None:
        out[2 * dirs : 2 * dirs + 8, :] = info[...]


def rows8(row):
    return jnp.broadcast_to(row, (8, LANE))


def lanes_of(table, index):
    return jnp.take_along_axis(table, index, axis=1, mode="promise_in_bounds")


def lookup(owner_row, tables, shards):
    low = rows8(owner_row & (LANE - 1))
    high = rows8(owner_row >> 7)
    out = jnp.zeros((8, LANE), f32)
    for table, shard in zip(tables, shards):
        out = jnp.where(high == shard, lanes_of(table, low), out)
    return out


def gather_corners(field, blocks, live_blocks, conn, base, corners, one_ref, by_matmul, v_ref):
    held = {(c, b): field(c, b) for c in range(3) for b in live_blocks}
    zero = jnp.zeros((8, LANE), f32)
    pairs = WIDE // LANE
    wides = blocks // pairs
    lines = []
    for w in range(wides):
        whole = jnp.concatenate(
            [
                jnp.concatenate([held.get((c, pairs * w + h), zero) for c in range(3)], axis=0)
                for h in range(pairs)
            ],
            axis=1,
        )
        lines += list(halves(whole))
    found = lax.dot_general(
        jnp.concatenate(lines, axis=0).astype(jnp.bfloat16),
        one_ref[:, : by_matmul * LANE],
        (((1,), (0,)), ((), ())),
        preferred_element_type=f32,
    )
    for n in range(by_matmul, corners):
        row = conn[n : n + 1, :] - base
        low = rows8(row & (LANE - 1))
        high = rows8(row >> 7)
        tests = {b: high == b for b in live_blocks}
        for c in range(3):
            acc = zero
            for b in live_blocks:
                acc = jnp.where(tests[b], lanes_of(held[c, b], low), acc)
            v_ref[c * corners + n] = acc
    for n in range(by_matmul):
        high = rows8((conn[n : n + 1, :] - base) >> 8)
        lanes = slice(n * LANE, (n + 1) * LANE)
        for c in range(3):
            acc = None
            for w in range(wides):
                top = 48 * w + 8 * c
                both = found[top : top + 8, lanes] + found[top + 24 : top + 32, lanes]
                acc = both if acc is None else jnp.where(high == w, both, acc)
            v_ref[c * corners + n] = acc


def windows(corners):
    return list(range(0, corners - 8, 8)) + [corners - 8]


def gather_rows(table, live_blocks, conn, base, start):
    index = conn[start : start + 8, :] - base
    low = index & (LANE - 1)
    high = index >> 7
    acc = jnp.zeros((8, LANE), f32)
    for b in live_blocks:
        acc = jnp.where(high == b, lanes_of(rows8(table(b)), low), acc)
    return acc


def factored_product(k_ref, speed, beta, kv_ref, o_ref, corners, group, ready):
    starts = windows(corners)

    def step(block, carry):
        i0 = block * group
        ready(block)
        for t in range(group):
            for w, start in enumerate(starts):
                kv = None
                for c in range(3):
                    term = k_ref[i0 + t, c * corners + start : c * corners + start + 8, :] * speed[c][w]
                    kv = term if kv is None else kv + term
                kv_ref[t, start : start + 8, :] = kv
        for t in range(group):
            acc = None
            for n in range(corners):
                term = rows8(kv_ref[t, n : n + 1, :]) * beta[n]
                acc = term if acc is None else acc + term
            o_ref[i0 + t] = acc
        return carry

    lax.fori_loop(0, 3 * corners // group, step, 0)


def product(k_ref, v_ref, o_ref, size, group, ready=None):
    count = size // group
    for i in range(size):
        o_ref[i] = jnp.zeros((8, LANE), f32)

    def step(block, carry):
        i0 = block * group
        if ready is not None:
            ready(block)
        vi = [v_ref[i0 + t] for t in range(group)]
        acc = [jnp.zeros((8, LANE), f32) for _ in range(group)]
        for t in range(group):
            for u in range(group):
                acc[t] = acc[t] + rows8(k_ref[i0 + t, pl.ds(i0 + u, 1), :]) * vi[u]
        for d in range(1, count // 2 + 1):
            j0 = jnp.where(block + d >= count, block + d - count, block + d) * group
            vj = [v_ref[j0 + u] for u in range(group)]
            far = [o_ref[j0 + u] for u in range(group)]
            for t in range(group):
                for u in range(group):
                    k = rows8(k_ref[i0 + t, pl.ds(j0 + u, 1), :])
                    acc[t] = acc[t] + k * vj[u]
                    far[u] = far[u] + k * vi[t]
            for u in range(group):
                o_ref[j0 + u] = far[u]
        for t in range(group):
            o_ref[i0 + t] += acc[t]
        return carry

    lax.fori_loop(0, count, step, 0)


def halves(x):
    high = x.astype(jnp.bfloat16).astype(f32)
    return high, x - high


def scatter_corners(o_ref, live, conn, base, corners, blocks, a_ref, one_ref):
    live = live[...] > 0
    wides = blocks * LANE // WIDE
    for first in range(0, corners, 2):
        some = range(first, min(first + 2, corners))
        lanes = slice(first * LANE, (first + len(some)) * LANE)
        high = jnp.concatenate([jnp.where(live, rows8((conn[n : n + 1, :] - base) >> 8), -1) for n in some], axis=1)
        parts = [halves(jnp.concatenate([o_ref[c * corners + n] for n in some], axis=1)) for c in range(3)]
        pieces = [p[k].astype(jnp.bfloat16) for k in range(2) for p in parts]
        for b in range(wides):
            here = (high == b).astype(f32).astype(jnp.bfloat16)
            for i, piece in enumerate(pieces):
                top = 48 * b + 8 * i
                a_ref[top : top + 8, lanes] = piece * here
    res = lax.dot_general(
        a_ref[...], one_ref[...], (((1,), (1,)), ((), ())), preferred_element_type=f32
    )
    sums = []
    for b in range(wides):
        both = res[b * 48 : b * 48 + 24] + res[b * 48 + 24 : b * 48 + 48]
        sums += [both[:, h * LANE : (h + 1) * LANE] for h in range(WIDE // LANE)]
    return sums


def forward_kernel(cfg, *refs):
    subs, order, masks, nodes, basal, corners, curves = cfg
    steps = len(masks)
    held, got, (low_b, mid_b) = refs[0], refs[1 : 1 + steps], refs[1 + steps : 3 + steps]
    velocity, owner, weight, kmat_hbm, _, conn, one_ref, live = refs[3 + steps : 11 + steps]
    ext, edge_out, info_out, kmat = refs[11 + steps : 15 + steps]
    swaps_out = refs[15 + steps : 15 + 2 * steps]
    v_ref, o_ref, a_ref, kv_ref, sems = refs[15 + 2 * steps :]
    s = lax.axis_index("sub")

    def piece(block):
        part = pl.ds(block * GROUP, GROUP)
        return pltpu.make_async_copy(kmat_hbm.at[part], kmat.at[part], sems.at[block])

    for block in range(EARLY, 3 * corners // GROUP):
        piece(block).start()

    def ready(block):
        @pl.when(block >= EARLY)
        def _():
            piece(block).wait()

    half = subs // 2
    own_blocks = nodes // LANE
    blocks = own_blocks + 2
    last = s == subs - 1
    dirs = 8 * half

    info = low_b[dirs : dirs + 8, :]
    for t in range(steps):
        rows = got[t].shape[0]
        chain = (s & (2 * (1 << t) - 1)) == (1 << t) - 1
        info = jnp.where(chain, got[t][rows - 8 : rows, :], info)
    info = jnp.where(last, low_b[dirs : dirs + 8, :], info)
    info_out[...] = info

    mine = [held[8 * q : 8 * q + 8, :] for q in range(half)]
    mine += [got[-1][8 * q : 8 * q + 8, :] for q in range(half)]
    shards = [s ^ r for r in order]
    theirs = [low_b[8 * q : 8 * q + 8, :] for q in range(half)]
    theirs += [mid_b[8 * q : 8 * q + 8, :] for q in range(half)]
    their_shards = [order[q] for q in range(half)] + [half ^ order[q] for q in range(half)]
    next_tables = [jnp.where(last, b, a) for a, b in zip(mine, theirs)]
    next_shards = [jnp.where(last, b, a) for a, b in zip(shards, their_shards)]

    base = nodes - BAND
    live_blocks = [1 + b for b in range(basal // LANE)] + [blocks - 1]
    beta = {}
    for b in range(basal // LANE):
        beta[1 + b] = lookup(owner[:, b * LANE : (b + 1) * LANE], mine, shards)
    beta[blocks - 1] = lookup(info[3:4, :].astype(jnp.int32), next_tables, next_shards)

    def speed_row(c, b):
        return info[c : c + 1, :] if b == blocks - 1 else velocity[c : c + 1, (b - 1) * LANE : b * LANE]

    speed = [
        [gather_rows(functools.partial(speed_row, c), live_blocks, conn, base, start) for start in windows(corners)]
        for c in range(3)
    ]
    for n in range(corners):
        row = conn[n : n + 1, :] - base
        low = rows8(row & (LANE - 1))
        high = rows8(row >> 7)
        acc = jnp.zeros((8, LANE), f32)
        for b in live_blocks:
            acc = jnp.where(high == b, lanes_of(beta[b], low), acc)
        v_ref[n] = acc
    factored_product(kmat, speed, [v_ref[n] for n in range(corners)], kv_ref, o_ref, corners, GROUP, ready)
    sums = scatter_corners(o_ref, live, conn, base, corners, blocks, a_ref, one_ref)
    for b in range(blocks):
        ext[:, b * LANE : (b + 1) * LANE] = sums[b]
    pad = jnp.zeros((5, LANE), f32)
    none = jnp.zeros((8, LANE), f32)
    w_low = jnp.concatenate([weight[:, 0:BAND], pad], axis=0)
    w_high = jnp.concatenate([weight[:, nodes - BAND : nodes], pad], axis=0)
    before = ((sums[0], none), (sums[1], w_low))
    after = ((sums[blocks - 2], w_high), (sums[blocks - 1], none))
    g = lax.axis_index("curve")
    goes_up = last | ((s == half - 1) & (g > 0))
    goes_down = (s == 0) | ((s == half) & (g < curves - 1))
    for col in range(2):
        for part, rows in ((0, slice(0, 24)), (1, slice(24, 32))):
            down, up = before[col][part], after[col][part]
            lanes = slice(col * LANE, (col + 1) * LANE)
            for t in range(steps):
                swaps_out[t][rows, lanes] = jnp.where((s & (1 << t)) == 0, up, down)
            edge_out[rows, lanes] = jnp.where(goes_up, up, jnp.where(goes_down, down, 0.0))


def neighbours(s, edge, swaps, subs):
    prev = nxt = edge
    for t, got in enumerate(swaps):
        ones = (1 << t) - 1
        nxt = jnp.where((s & (2 * ones + 1)) == ones, got, nxt)
        prev = jnp.where((s & (2 * ones + 1)) == ones + 1, got, prev)
    nxt = jnp.where(s == subs - 1, edge, nxt)
    return prev, nxt


def adjoint_kernel(cfg, *refs):
    subs, order, masks, nodes, basal, corners, curves = cfg
    steps = len(masks)
    ext, edge_in, info, velocity, owner, weight, kmat, conn, one_ref, live = refs[:10]
    swaps_in = refs[10 : 10 + steps]
    n_out = 4 + steps
    outs = refs[10 + steps : 10 + steps + n_out]
    v_ref, o_ref, a_ref = refs[10 + steps + n_out :]
    own_out, inner_out, edge_out, far_out = outs[:4]
    dense_out = outs[4]
    band_outs = outs[5:]
    s = lax.axis_index("sub")
    half = subs // 2
    blocks = nodes // LANE + 2
    last = s == subs - 1
    base = nodes - BAND
    g = lax.axis_index("curve")
    by_ends = ((g == 0) & (s == half)) | ((g == curves - 1) & (s == half - 1))
    middle = jnp.where(by_ends, swaps_in[-1][...], edge_in[...])
    prev, nxt = neighbours(s, edge_in[...], [x[...] for x in swaps_in[:-1]] + [middle], subs)

    values = {}
    for c in range(3):
        part = slice(8 * c, 8 * c + 8)
        for b in range(blocks):
            x = ext[part, b * LANE : (b + 1) * LANE]
            if b == 0:
                x = (x + prev[part, 0:LANE]) * rows8(prev[24 + c : 25 + c, 0:LANE])
            elif b == blocks - 1:
                x = (x + nxt[part, LANE:]) * rows8(nxt[24 + c : 25 + c, LANE:])
            else:
                if b == 1:
                    x = x + prev[part, LANE:]
                if b == blocks - 2:
                    x = x + nxt[part, 0:LANE]
                x = x * rows8(weight[c : c + 1, (b - 1) * LANE : b * LANE])
            values[c, b] = x
    gather_corners(lambda c, b: values[c, b], blocks, range(blocks), conn, base, corners, one_ref, ADJOINT_MATMUL, v_ref)
    product(kmat, v_ref, o_ref, 3 * corners, GROUP)
    sums = scatter_corners(o_ref, live, conn, base, corners, blocks, a_ref, one_ref)
    for b in range(1, blocks - 1):
        own_out[:, (b - 1) * LANE : b * LANE] = sums[b]
    lower, upper = sums[0], sums[blocks - 1]

    n_basal = basal // LANE
    terms, owners = [], []
    for b in range(n_basal):
        terms.append(
            sum(
                rows8(velocity[c : c + 1, b * LANE : (b + 1) * LANE]) * sums[1 + b][8 * c : 8 * c + 8]
                for c in range(3)
            )
        )
        owners.append(owner[:, b * LANE : (b + 1) * LANE])
    beyond = sum(rows8(info[c : c + 1, :]) * upper[8 * c : 8 * c + 8] for c in range(3))
    terms.append(jnp.where(last, 0.0, beyond))
    owners.append(info[3:4, :].astype(jnp.int32))
    across = jnp.where(last, beyond, 0.0)
    sub_iota = lax.broadcasted_iota(jnp.int32, (LANE, LANE), 0)
    one = jnp.concatenate(
        [
            (jnp.broadcast_to(o & (LANE - 1), (LANE, LANE)) == sub_iota).astype(f32).astype(jnp.bfloat16)
            for o in owners
        ],
        axis=1,
    )
    split = [halves(t) for t in terms]
    split_across = halves(across)
    zero = jnp.zeros((8, LANE), f32)
    lines = []
    for r in order:
        here = [rows8(o >> 7) == (s ^ r) for o in owners]
        for piece in range(2):
            lines.append(
                jnp.concatenate([jnp.where(h, t[piece], 0.0) for h, t in zip(here, split)], axis=1)
            )
    for q in range(subs):
        shard = order[q] if q < half else half ^ order[q - half]
        here = rows8(owners[-1] >> 7) == shard
        for piece in range(2):
            lines.append(
                jnp.concatenate(
                    [zero] * n_basal + [jnp.where(here, split_across[piece], 0.0)], axis=1
                )
            )
    res = lax.dot_general(
        jnp.concatenate(lines, axis=0).astype(jnp.bfloat16),
        one,
        (((1,), (1,)), ((), ())),
        preferred_element_type=f32,
    )
    dense = [res[16 * q : 16 * q + 8] + res[16 * q + 8 : 16 * q + 16] for q in range(2 * subs)]
    rows = 8 * half
    g = lax.axis_index("curve")
    ends = (s == 0) | last
    broken = ((g == 0) & (s == half - 1)) | ((g == curves - 1) & (s == half))
    by_edge = ~(ends | broken)
    by_inner = ends | broken
    for q in range(half):
        part = slice(8 * q, 8 * q + 8)
        dense_out[part, :] = dense[q]
        far_out[part, :] = dense[subs + half + q]
        edge_out[part, :] = jnp.where(last, dense[subs + q], jnp.where(by_edge, dense[half + q], 0.0))
        inner_out[part, :] = jnp.where(by_inner, dense[half + q], 0.0)
    middle = jnp.where(s == half - 1, upper, jnp.where(s == half, lower, 0.0))
    tail = slice(rows, rows + 24)
    edge_out[tail, :] = jnp.where(last, upper, jnp.where(s == 0, lower, jnp.where(by_edge, middle, 0.0)))
    inner_out[tail, :] = jnp.where(broken, middle, 0.0)
    for t, band in enumerate(band_outs):
        up = (s & (1 << t)) == 0
        band[...] = jnp.where(up, upper, lower)


def relay_kernel(cfg, far, inner, out):
    subs, _, _, _, _, _, curves = cfg
    rows = far.shape[0]
    forward = (lax.axis_index("sub") == subs // 2) & (lax.axis_index("curve") < curves - 1)
    out[0:rows, :] = jnp.where(forward, far[...], inner[0:rows, :])
    out[rows:, :] = inner[rows:, :]


def shrink_kernel(first, *refs):
    if first:
        held, got, edge, band, msg, left = refs
    else:
        held, got, band, msg, left = refs
    rows = held.shape[0]
    total = held[...] + got[0:rows, :]
    if first:
        total = total + edge[0:rows, :]
    keep = rows // 2
    left[...] = total[0:keep]
    msg[0:keep, :] = total[keep:]
    msg[keep : keep + 24, :] = band[...]


def finish_kernel(cfg, *refs):
    subs, _, masks, nodes, _, _, _ = cfg
    steps = len(masks)
    own, held, edge, inner = refs[:4]
    got = refs[4 : 3 + steps]
    gradient, field = refs[3 + steps :]
    s = lax.axis_index("sub")
    gradient[...] = held[...] + got[0][0:8, :]
    tail = slice(edge.shape[0] - 24, edge.shape[0])
    far = edge[tail, :] + inner[tail, :]
    bands = [g[g.shape[0] - 24 :, :] for g in got] + [far]
    prev, nxt = neighbours(s, far, bands, subs)
    field[:, 0:LANE] = own[:, 0:LANE] + prev
    field[:, LANE : nodes - LANE] = own[:, LANE : nodes - LANE]
    field[:, nodes - LANE :] = own[:, nodes - LANE :] + nxt


def shape(*dims):
    return jax.ShapeDtypeStruct(dims, f32)


def local(curves, subs, direction, base_velocity, weight, element_matrix, connectivity, element_count, basal_owner):
    order, masks = xor_order(subs)
    half = subs // 2
    nodes = base_velocity.shape[1]
    basal = basal_owner.shape[0]
    corners, elems = connectivity.shape
    size = 3 * corners
    blocks = nodes // LANE + 2
    cfg = (subs, order, masks, nodes, basal, corners, curves)
    owner = basal_owner.reshape(1, basal)

    def call(kernel, out_shape, scratch=(), mib=4, specs=None, cost=None, alias={}):
        def run(*args):
            args = [
                pltpu.with_memory_space_constraint(x, pltpu.HBM) if specs and specs[i] is HBM else x
                for i, x in enumerate(args)
            ]
            return pl.pallas_call(
                kernel,
                out_shape=out_shape,
                in_specs=specs or [VMEM] * len(args),
                out_specs=jax.tree.map(lambda _: VMEM, out_shape),
                scratch_shapes=list(scratch),
                compiler_params=params(mib),
                cost_estimate=cost,
                input_output_aliases=alias,
            )(*args)

        return run

    def swap_sub(x, mask):
        return lax.ppermute(x, "sub", [(i, i ^ mask) for i in range(subs)])

    def swap_edge(x, place):
        return lax.ppermute(x, AX, edge_pairs(curves, subs, place))

    steps = len(masks)
    rows = 8 * half

    first = swap_sub(direction, masks[0])
    held, info, velocity, owner, conn, weight = call(
        pack_kernel,
        (
            shape(8, LANE),
            shape(8, LANE),
            shape(3, nodes),
            jax.ShapeDtypeStruct((1, basal), jnp.int32),
            jax.ShapeDtypeStruct((corners, elems), jnp.int32),
            shape(3, nodes),
        ),
        [pltpu.SemaphoreType.DMA((5,))],
        specs=[HBM] * 5,
        cost=pl.CostEstimate(flops=0, bytes_accessed=1 << 20, transcendentals=0),
    )(direction, base_velocity, owner, connectivity, weight)
    for mask in masks[1:-1]:
        held = call(functools.partial(grow_kernel, None), shape(2 * held.shape[0], LANE))(held, first)
        first = swap_sub(held, mask)
    held = call(grow_kernel, shape(2 * held.shape[0] + 8, LANE))(info, held, first)
    low_b = swap_edge(held, 0)
    mid_b = swap_edge(held, half)
    got = [swap_sub(info, mask) for mask in masks[:-1]]
    got.append(swap_sub(held, masks[-1]))

    kmat, one, live = call(
        functools.partial(prep_kernel, cfg),
        (
            shape(size, size, elems),
            jax.ShapeDtypeStruct((WIDE, corners * LANE), jnp.bfloat16),
            jax.ShapeDtypeStruct((8, LANE), jnp.int32),
        ),
        [pltpu.SemaphoreType.DMA((1,))],
        16,
        [VMEM, HBM, VMEM, SMEM],
        pl.CostEstimate(flops=0, bytes_accessed=8 << 20, transcendentals=0),
    )(held, element_matrix, conn, element_count)

    scratch = [
        pltpu.VMEM((size, 8, LANE), f32),
        pltpu.VMEM((size, 8, LANE), f32),
        pltpu.VMEM((48 * blocks * LANE // WIDE, corners * LANE), jnp.bfloat16),
    ]
    ext, edge, info, kmat, *swaps = call(
        functools.partial(forward_kernel, cfg),
        (shape(24, blocks * LANE), shape(32, 2 * LANE), shape(8, LANE), shape(size, size, elems))
        + (shape(32, 2 * LANE),) * steps,
        [pltpu.VMEM((corners, 8, LANE), f32)]
        + scratch[1:]
        + [pltpu.VMEM((GROUP, corners, LANE), f32), pltpu.SemaphoreType.DMA((size // GROUP,))],
        16,
        [VMEM] * (6 + steps) + [HBM] + [VMEM] * 4,
        alias={7 + steps: 3},
    )(held, *got, low_b, mid_b, velocity, owner, weight, element_matrix, kmat, conn, one, live)

    edge = lax.ppermute(edge, AX, edge_swap(curves, subs))
    swaps = [swap_sub(x, mask) for x, mask in zip(swaps[:-1], masks)] + [
        lax.ppermute(swaps[-1], AX, ends_swap(curves, subs))
    ]

    own, inner_msg, edge_msg, far_msg, dense, *bands = call(
        functools.partial(adjoint_kernel, cfg),
        (shape(24, nodes), shape(rows + 24, LANE), shape(rows + 24, LANE), shape(rows, LANE), shape(rows, LANE))
        + (shape(24, LANE),) * (steps - 1),
        scratch,
        16,
    )(ext, edge, info, velocity, owner, weight, kmat, conn, one, live, *swaps)

    far = swap_sub(far_msg, masks[-2])
    edge = lax.ppermute(edge_msg, AX, edge_swap(curves, subs))
    inner_msg = call(functools.partial(relay_kernel, cfg), shape(rows + 24, LANE))(far, inner_msg)
    inner = lax.ppermute(inner_msg, AX, inner_swap(curves, subs))
    got, extra, by_mask = inner, (edge,), [None] * (steps - 1)
    for t in range(steps - 2, -1, -1):
        keep = dense.shape[0] // 2
        msg, dense = call(
            functools.partial(shrink_kernel, bool(extra)), (shape(keep + 24, LANE), shape(keep, LANE))
        )(dense, got, *extra, bands[t])
        extra = ()
        got = by_mask[t] = swap_sub(msg, masks[t])
    gradient, field = call(functools.partial(finish_kernel, cfg), (shape(8, LANE), shape(24, nodes)))(
        own, dense, edge, inner, *by_mask
    )
    return gradient, field.reshape(3, 8, nodes)


def solution(mesh):
    curves, subs = mesh.shape["curve"], mesh.shape["sub"]
    in_specs = (
        P(None, AX),
        P(None, AX),
        P(None, AX),
        P(None, None, AX),
        P(None, AX),
        P(AX),
        P(AX),
    )
    out_specs = (P(None, AX), P(None, None, AX))
    return jax.shard_map(
        functools.partial(local, curves, subs), mesh=mesh, in_specs=in_specs, out_specs=out_specs, check_vma=False
    )
```
